32 devices in a mesh: groups: 2 (over x), asset: 16 (over z, y, core).
Axes of the slice: x: 2, y: 2, z: 4, core: 2. Of those that a mesh axis runs over, the one named last changes fastest.
Arguments:
- scen_draws: bfloat16 [8192, 256], P(('groups', 'asset')), parts along dimension 0, may hold values from -4 to 4
- factor_mix: bfloat16 [256, 256], replicated, may hold values from -0.375 to 0.375
- loadings: bfloat16 [32768, 256], P(('groups', 'asset')), parts along dimension 0, may hold values from -0.375 to 0.375
- convexity: float32 [32768], P(('groups', 'asset')), parts along dimension 0, may hold values from -0.6 to 0.6
- holdings: float32 [32768], P(('groups', 'asset')), parts along dimension 0, may hold values from -0.22097087 to 0.22097087
- desk_map: int32 [32768], P(('groups', 'asset')), parts along dimension 0, may hold values from 0 to 127
- ranks: int32 [8192], P('groups'), parts along dimension 0, may hold values from 0 to 4095, each once
- desk_prices: float32 [256], P('groups'), parts along dimension 0, may hold values from -5 to 5
Outputs:
- allocation: float32 [256], P('groups'), parts along dimension 0
- grad_loadings: float32 [32768, 256], P(('groups', 'asset')), parts along dimension 0
- grad_convexity: float32 [32768], P(('groups', 'asset')), parts along dimension 0
The draws below stay inside these ranges and needn't reach their ends.
There are 2 independent parts, one for each index of `groups`. The reference program is written for one: setup_inputs(seed, part) draws one part's arguments, and reference() takes and returns one part's arrays. A program takes and returns all parts, laid end to end along the dimension named above; an argument that names none is the same for every part. Nothing has to cross between parts.
All inputs are finite; a program needn't handle non-finite values.
Results may differ from the reference program's by a relative error of at most 0.0029.
Values may be sent and summed in bfloat16 or wider, within the bound.
A program may use at most 64 MiB of HBM per device.

```python
import math
import jax
import jax.numpy as jnp
from jax import lax

F = 256
DESKS = 128
SCEN = 4096
ASSETS = 16384
BAND = 32
CENTER = 166


def draw_scen_draws(key, part):
    position = jnp.arange(SCEN, dtype=jnp.float32) / SCEN
    base = jax.random.normal(key, (SCEN, F), jnp.float32)
    growth = jnp.exp((position - 0.5) * math.log(3.0))
    return jnp.clip(base * growth[:, None], -4.0, 4.0).astype(jnp.bfloat16)


def draw_holdings(key, part):
    position = jnp.arange(ASSETS, dtype=jnp.float32) / ASSETS
    base = jax.random.normal(key, (ASSETS,), jnp.float32)
    growth = jnp.exp((position - 0.5) * math.log(3.0))
    return jnp.clip(base * growth, -2.5, 2.5) / math.sqrt(ASSETS // DESKS)


def place_ends(entries, stream_key, low, top_value):
    extent = entries.shape
    index_at = [jax.random.randint(jax.random.fold_in(stream_key, axis), (), 0, extent[axis]) for axis in range(len(extent))]
    entries = entries.at[tuple(index_at)].set(low)
    longest = extent.index(max(extent))
    index_at[longest] = (index_at[longest] + 1) % extent[longest]
    return entries.at[tuple(index_at)].set(top_value)


def steps_of(rng, dims, cuts, smallest, largest):
    def one(dim, parts):
        heights = jax.random.uniform(jax.random.fold_in(jax.random.fold_in(rng, 6), dim), (parts,), jnp.float32, smallest / len(cuts), largest / len(cuts))
        return jnp.repeat(jnp.exp(heights), dims[dim] // parts).reshape((-1,) + (1,) * (len(dims) - dim - 1))

    factor_of = one(*cuts[0])
    for cut in cuts[1:]:
        factor_of = factor_of * one(*cut)
    return factor_of


def normal_values(key, shape, deviation, reach, pieces=(), kind=jnp.bfloat16):
    array = jax.random.normal(key, shape, jnp.float32) * deviation
    if len(pieces) > 0:
        array = steps_of(key, shape, pieces, -0.22, 0.18) * array
    return jnp.clip(array, min=-reach, max=reach).astype(kind)


def setup_inputs(seed: int = 0, part: int = 0) -> dict:
    seeds = jax.random.split(jax.random.key(seed), 9)
    part_splits = jax.random.split(jax.random.fold_in(seeds[8], part), 9)
    scen_draws = draw_scen_draws(jax.random.fold_in(jax.random.fold_in(seeds[8], part), 71), part)
    factor_mix = normal_values(seeds[1], (F, F), F ** -0.5, 0.375)
    loadings = normal_values(part_splits[2], (ASSETS, F), F ** -0.5, 0.375, ((0, 16),))
    convexity = jnp.clip(jax.random.uniform(part_splits[3], (ASSETS,), jnp.float32, -0.6, 0.6) * steps_of(part_splits[3], (ASSETS,), ((0, 16),), -0.4, 0.0), -0.6, 0.6)
    holdings = draw_holdings(jax.random.fold_in(jax.random.fold_in(seeds[8], part), 71), part)
    desk_map = place_ends(jax.random.randint(part_splits[5], (ASSETS,), 0, DESKS), jax.random.fold_in(part_splits[5], 1), 0, DESKS - 1).astype(jnp.int32)
    ranks = jax.random.permutation(part_splits[6], SCEN).astype(jnp.int32)
    desk_prices = normal_values(part_splits[7], (DESKS,), 1.0, 5.0, (), jnp.float32)
    return dict(scen_draws=scen_draws, factor_mix=factor_mix, loadings=loadings, convexity=convexity, holdings=holdings, desk_map=desk_map, ranks=ranks, desk_prices=desk_prices)


def smooth_bend(value):
    return jnp.logaddexp(value, -value) - math.log(2.0)

def rank_kernel(ranks, scenarios):
    centre = jnp.float32(CENTER)
    spread = jnp.float32(BAND)
    offsets = (ranks.astype(jnp.float32) - centre) / spread
    every = (jnp.arange(scenarios, dtype=jnp.float32) - centre) / spread
    return jnp.exp(-0.5 * offsets * offsets) / jnp.sum(jnp.exp(-0.5 * every * every))

def cotangent_of(weights, weight_total, slopes, smoothing, kernel, grad_quant, grad_band, centred, prices, scenarios):
    grad_loss = slopes / smoothing + kernel * grad_quant + grad_band * 0.09 * centred / (scenarios * smoothing)
    return (scenarios * (-weights[:, None] * prices[None, :] / weight_total - grad_loss[:, None])).astype(jnp.bfloat16)

def tail_terms(desk_pnl, ranks, prices):
    scenarios = desk_pnl.shape[0]
    losses = -lax.optimization_barrier(jnp.sum(desk_pnl, axis=1))
    kernel = rank_kernel(ranks, scenarios)
    quantile = jnp.sum(kernel * losses)
    average = jnp.mean(losses)
    centred = losses - average
    smoothing = 0.3 * jnp.sqrt(jnp.mean(centred * centred) + 1e-06)
    scores = (losses - quantile) / smoothing
    weights = jax.nn.sigmoid(scores)
    weight_total = jnp.sum(weights)
    valued = lax.optimization_barrier(jnp.sum(desk_pnl * prices[None, :], axis=1))
    objective = -jnp.sum(weights * valued) / weight_total
    allocation = -lax.optimization_barrier(jnp.sum(weights[:, None] * desk_pnl, axis=0)) / weight_total
    slopes = (-valued - objective) / weight_total * weights * (1.0 - weights)
    grad_quant = -jnp.sum(slopes) / smoothing
    grad_band = -jnp.sum(slopes * scores) / smoothing
    cotangent = cotangent_of(weights, weight_total, slopes, smoothing, kernel, grad_quant, grad_band, centred, prices, scenarios)
    return (cotangent, allocation)

def exposure_of(shock_rows, loadings):
    return lax.dot_general(shock_rows, loadings, (((1,), (1,)), ((), ())), preferred_element_type=jnp.float32)

def reference(scen_draws, factor_mix, loadings, convexity, holdings, desk_map, ranks, desk_prices):
    shocks = jnp.dot(scen_draws, factor_mix, preferred_element_type=jnp.float32).astype(jnp.bfloat16)
    block_rows = math.gcd(SCEN, 256)
    shock_blocks = shocks.reshape((-1, block_rows, F))

    def forward(shock_block):
        exposure = exposure_of(shock_block, loadings)
        held = (holdings * (exposure + convexity * smooth_bend(exposure))).astype(jnp.bfloat16)
        summed = jax.ops.segment_sum(held.astype(jnp.float32).T, desk_map, num_segments=DESKS)
        return summed.T
    desk_pnl = lax.map(forward, shock_blocks).reshape((SCEN, DESKS))
    cotangent, allocation = tail_terms(desk_pnl, ranks, desk_prices)
    cot_blocks = cotangent.reshape((-1, block_rows, DESKS))

    def backward(state, inputs):
        shock_block, cot_block = inputs
        exposure = exposure_of(shock_block, loadings)
        held = holdings * cot_block[:, desk_map].astype(jnp.float32)
        grad_exposure = (held * (1.0 + convexity * jnp.tanh(exposure))).astype(jnp.bfloat16)
        grad_load = state[0] + lax.dot_general(grad_exposure, shock_block, (((0,), (0,)), ((), ())), preferred_element_type=jnp.float32)
        grad_conv = state[1] + lax.optimization_barrier(jnp.sum(held * smooth_bend(exposure), axis=0))
        return ((grad_load, grad_conv), None)
    initial = (jnp.zeros((ASSETS, F), jnp.float32), jnp.zeros((ASSETS,), jnp.float32))
    final, ignored = lax.scan(backward, initial, (shock_blocks, cot_blocks))
    grad_load, grad_conv = final
    squares = jnp.sum(grad_load * grad_load) + jnp.sum(grad_conv * grad_conv)
    factor = lax.rsqrt(squares / (ASSETS * (F + 1)) + 1e-06)
    return (allocation, grad_load * factor, grad_conv * factor)
```

```python
import functools
import math

import jax
import jax.numpy as jnp
from jax import lax
from jax.experimental import pallas as pl
from jax.experimental.pallas import tpu as pltpu
from jax.sharding import PartitionSpec as P

DESKS = 128
BAND = 32
CENTER = 166
MESH = pl.DeviceIdType.MESH
F32 = jnp.float32
BF16 = jnp.bfloat16
NT = (((1,), (1,)), ((), ()))


def dot(left, right):
    return jnp.dot(left, right, preferred_element_type=F32)


def dot_nt(left, right):
    return lax.dot_general(left, right, NT, preferred_element_type=F32)


def halves(value):
    high = value.astype(BF16).astype(F32)
    return high, value - high


def stack_rows(rows, count):
    width = rows[0].shape[1]
    if count > len(rows):
        rows = list(rows) + [jnp.zeros((count - len(rows), width), F32)]
    return jnp.concatenate(rows, axis=0)


def total(value):
    return jnp.sum(jnp.sum(value, axis=1, keepdims=True), axis=0, keepdims=True)


def position_of(chip, chips, folded):
    if not folded:
        return chip
    return chip // 2 + (chip % 2) * (chips - 1 - 2 * (chip // 2))


def chip_at(position, chips, folded):
    position = (position + chips) % chips
    if not folded:
        return position
    back = position // (chips // 2)
    return 2 * position + back * (2 * chips - 1 - 4 * position)


def kernel(
    n,
    folded,
    draws_ref,
    mix_ref,
    load_ref,
    conv_ref,
    hold_ref,
    desk_ref,
    ranks_ref,
    prices_ref,
    alloc_ref,
    grad_ref,
    gconv_ref,
    landed,
    shocks,
    tanhs,
    bends,
    scaled,
    table,
    columns,
    first_rows,
    part,
    gathered,
    sums,
    loss_all,
    valued_all,
    stat_rows,
    finals,
    ring_send,
    ring_recv,
    pair_send,
    pair_recv,
    part_send,
    part_recv,
    sums_send,
    sums_recv,
    fin_send,
    fin_recv,
    own_sem,
):
    me = lax.axis_index("asset")
    chips = n // 2
    core = me % 2
    chip = me // 2
    where = position_of(chip, chips, folded)
    partner = chip * 2 + (1 - core)
    right = chip_at(where + 1, chips, folded) * 2 + core
    left = chip_at(where - 1, chips, folded) * 2 + core
    rows, factors = draws_ref.shape
    block = 2 * rows
    scenarios = rows * n
    assets = load_ref.shape[0]
    tile = math.gcd(assets, 256)
    last = chips // 2
    half = rows // 2

    barrier = pltpu.get_barrier_semaphore()
    for other in (right, left, partner):
        pl.semaphore_signal(barrier, inc=1, device_id={"asset": other}, device_id_type=MESH)
    pl.semaphore_wait(barrier, 3)

    def shard_at(step):
        return chip_at(where + step, chips, folded) * 2 + core

    def ring_copy(direction, step):
        shard = shard_at(-direction * (step - 1))
        lane = 0 if direction == 1 else 1
        source = draws_ref if step == 1 else landed.at[shard]
        target = landed.at[shard]
        if step == last:
            piece = pl.ds(0 if direction == 1 else half, half)
            source, target = source.at[piece], target.at[piece]
        return pltpu.make_async_remote_copy(
            src_ref=source,
            dst_ref=target,
            send_sem=ring_send.at[lane, step - 1],
            recv_sem=ring_recv.at[lane, step - 1],
            device_id={"asset": right if direction == 1 else left},
            device_id_type=MESH,
        )

    def pair_copy(step):
        shard = shard_at(step)
        source = draws_ref if step == 0 else landed.at[shard]
        return pltpu.make_async_remote_copy(
            src_ref=source,
            dst_ref=landed.at[shard],
            send_sem=pair_send.at[step + last],
            recv_sem=pair_recv.at[step + last],
            device_id={"asset": partner},
            device_id_type=MESH,
        )

    started = []

    def start(copy):
        copy.start()
        started.append(copy)
        return copy

    ring = {}
    for direction in (1, -1):
        ring[direction, 1] = start(ring_copy(direction, 1))
    pair = {0: start(pair_copy(0))}
    own = pltpu.make_async_copy(draws_ref, landed.at[me], own_sem)
    own.start()

    conv = conv_ref[...]
    hold = hold_ref[...]
    desk = desk_ref[...]
    same = lax.broadcasted_iota(jnp.int32, (DESKS, assets), 0) == desk
    table[...] = same.astype(F32).astype(BF16)
    price_high, price_rest = halves(prices_ref[...])
    price_mid, price_low = halves(price_rest)
    price_rows = stack_rows([price_high, price_mid, price_low], 16).astype(BF16)
    price = jnp.sum(dot(price_rows, table[...]), axis=0, keepdims=True)
    columns[...] = jnp.transpose(stack_rows([conv, hold, price], 128))
    linear = dot(
        stack_rows([*halves(hold), *halves(hold * price)], 16).astype(BF16), load_ref[...]
    )
    linear_loss = linear[0:1] + linear[1:2]
    linear_value = linear[2:3] + linear[3:4]
    linear_rows = stack_rows([*halves(linear_loss), *halves(linear_value)], 16).astype(BF16)
    bent = hold * conv
    first_rows[...] = stack_rows([*halves(bent), *halves(bent * price)], 16).astype(BF16)

    def forward(step):
        place = chip_at(where + step, chips, folded)
        draws = landed[pl.ds(place * 2, 2)].reshape(block, factors)
        shock = dot(draws, mix_ref[...]).astype(BF16)
        at = pl.multiple_of(place * block, block)
        shocks[pl.ds(at, block), :] = shock
        result = dot_nt(linear_rows, shock)
        for first in range(0, assets, tile):
            exposure = dot_nt(load_ref[pl.ds(first, tile), :], shock)
            tanhs[pl.ds(first, tile), pl.ds(at, block)] = jnp.tanh(exposure).astype(BF16)
            size = jnp.abs(exposure)
            bend = (size + jnp.log(1.0 + jnp.exp(-2.0 * size)) - math.log(2.0)).astype(BF16)
            bends[pl.ds(first, tile), pl.ds(at, block)] = bend
            result = result + dot(first_rows[:, first : first + tile], bend)
        loss = -(result[0:1] + result[1:2])
        value = result[2:3] + result[3:4]
        both = jnp.concatenate([loss, value], axis=0)
        part[place * 2] = both[:, 0:rows]
        part[place * 2 + 1] = both[:, rows:block]

    own.wait()
    pair[0].wait_recv()
    pending = [0]
    for step in range(1, last + 1):
        arrived = (-step, step) if step < last else (step,)
        for direction in (1, -1):
            ring[direction, step].wait_recv()
            if step < last:
                ring[direction, step + 1] = start(ring_copy(direction, step + 1))
                pair[-direction * step] = start(pair_copy(-direction * step))
        if step == last:
            pair[last] = start(pair_copy(last))
        for ready in pending:
            forward(ready)
        for ready in arrived:
            pair[ready].wait_recv()
        pending = arrived
    for ready in pending:
        forward(ready)
    for copy in started:
        copy.wait_send()

    def to_all(source, target, send_sem, recv_sem):
        copies = []
        for offset in range(1, n):
            other = (me + offset) % n
            copies.append(
                pltpu.make_async_remote_copy(
                    src_ref=source(other),
                    dst_ref=target(offset),
                    send_sem=send_sem.at[offset],
                    recv_sem=recv_sem.at[offset],
                    device_id={"asset": other},
                    device_id_type=MESH,
                )
            )
        for copy in copies:
            copy.start()
        return copies

    copies = to_all(lambda other: part.at[other], lambda offset: gathered.at[offset], part_send, part_recv)
    mine = part[me]
    for copy in copies:
        copy.wait()
    for offset in range(1, n):
        mine = mine + gathered[offset]
    sums[me] = mine
    copies = to_all(lambda other: sums.at[me], lambda offset: sums.at[me], sums_send, sums_recv)
    for copy in copies:
        copy.wait()
    for device in range(n):
        entry = sums[device]
        loss_all[pl.ds(device, 1), :] = entry[0:1]
        valued_all[pl.ds(device, 1), :] = entry[1:2]

    losses = loss_all[...]
    valued = valued_all[...]
    offsets = (ranks_ref[...].astype(F32) - CENTER) / BAND
    counter = (
        lax.broadcasted_iota(jnp.int32, (n, rows), 0) * rows
        + lax.broadcasted_iota(jnp.int32, (n, rows), 1)
    )
    every = (counter.astype(F32) - CENTER) / BAND
    bell = jnp.exp(-0.5 * offsets * offsets) / total(jnp.exp(-0.5 * every * every))
    quantile = total(bell * losses)
    centred = losses - total(losses) / scenarios
    smoothing = 0.3 * jnp.sqrt(total(centred * centred) / scenarios + 1e-06)
    scores = (losses - quantile) / smoothing
    weights = jax.nn.sigmoid(scores)
    weight_total = total(weights)
    objective = -total(weights * valued) / weight_total
    slopes = (-valued - objective) / weight_total * weights * (1.0 - weights)
    grad_quant = -total(slopes) / smoothing
    grad_band = -total(slopes * scores) / smoothing
    grad_loss = (
        slopes / smoothing
        + bell * grad_quant
        + grad_band * 0.09 * centred / (scenarios * smoothing)
    )
    share = weights * (scenarios / weight_total)
    grad_loss = scenarios * grad_loss

    wide = -(-rows // 128) * 128
    upright = stack_rows([share, grad_loss], -(-2 * n // 128) * 128)
    if wide > rows:
        upright = jnp.concatenate(
            [upright, jnp.zeros((upright.shape[0], wide - rows), F32)], axis=1
        )
    upright = jnp.transpose(upright)
    for device in range(n):
        piece = shocks[device * rows : (device + 1) * rows, :].astype(F32)
        for side in range(2):
            scale = upright[0:rows, side * n + device : side * n + device + 1]
            scaled[
                device * rows : (device + 1) * rows, side * factors : (side + 1) * factors
            ] = (piece * scale).astype(BF16)
    pieces = [*halves(share), *halves(grad_loss)]
    for place in range(chips):
        lines = [
            jnp.concatenate(
                [piece[2 * place : 2 * place + 1], piece[2 * place + 1 : 2 * place + 2]], axis=1
            )
            for piece in pieces
        ]
        stat_rows[:, place * block : (place + 1) * block] = stack_rows(lines, 16).astype(BF16)

    plain = dot(stat_rows[...], shocks[...])
    plain_share = plain[0:1] + plain[1:2]
    plain_loss = plain[2:3] + plain[3:4]
    plain_rows = stack_rows([*halves(plain_share)], 16).astype(BF16)

    squares = jnp.zeros((1, 1), F32)
    allocation = jnp.zeros((1, DESKS), F32)
    for first in range(0, assets, tile):
        span = slice(first, first + tile)
        both = dot(tanhs[span, :], scaled[...])
        conv_column = columns[span, 0:1]
        hold_column = columns[span, 1:2]
        price_column = columns[span, 2:3]
        raw = -hold_column * (
            price_column * (plain_share + conv_column * both[:, 0:factors])
            + (plain_loss + conv_column * both[:, factors:])
        )
        grad_ref[span, :] = raw
        squares = squares + total(raw * raw)
        sides = dot_nt(stat_rows[...], bends[span, :])
        side_share = sides[0:1] + sides[1:2]
        side_loss = sides[2:3] + sides[3:4]
        hold_row = hold_ref[:, span]
        raw_conv = -hold_row * (price[:, span] * side_share + side_loss)
        gconv_ref[:, span] = raw_conv
        squares = squares + total(raw_conv * raw_conv)
        linear_share = dot_nt(plain_rows, load_ref[span, :])
        using = hold_row * (
            linear_share[0:1] + linear_share[1:2] + conv_ref[:, span] * side_share
        )
        using_rows = stack_rows([*halves(using)], 16).astype(BF16)
        found = dot_nt(using_rows, table[:, span])
        allocation = allocation - (found[0:1] + found[1:2])
    finals[me] = stack_rows(
        [allocation * (1.0 / scenarios), jnp.broadcast_to(squares, (1, DESKS))], 8
    )
    copies = to_all(lambda other: finals.at[me], lambda offset: finals.at[me], fin_send, fin_recv)
    for copy in copies:
        copy.wait()
    final = finals[0]
    for device in range(1, n):
        final = final + finals[device]
    alloc_ref[...] = final[0:1]
    entries = assets * n * (factors + 1)
    factor = lax.rsqrt(final[1:2, 0:1] / entries + 1e-06)
    gconv_ref[...] = gconv_ref[...] * factor
    grad_ref[...] = grad_ref[...] * factor


def shards(
    folded, n, scen_draws, factor_mix, loadings, convexity, holdings, desk_map, ranks, desk_prices
):
    rows, factors = scen_draws.shape
    assets = loadings.shape[0]
    scenarios = rows * n
    last = n // 4
    dma = pltpu.SemaphoreType.DMA
    vmem = pl.BlockSpec(memory_space=pltpu.VMEM)
    allocation, grad_load, grad_conv = pl.pallas_call(
        functools.partial(kernel, n, folded),
        out_shape=(
            jax.ShapeDtypeStruct((1, DESKS), F32),
            jax.ShapeDtypeStruct((assets, factors), F32),
            jax.ShapeDtypeStruct((1, assets), F32),
        ),
        in_specs=[vmem] * 8,
        out_specs=(vmem,) * 3,
        scratch_shapes=[
            pltpu.VMEM((n, rows, factors), BF16),
            pltpu.VMEM((scenarios, factors), BF16),
            pltpu.VMEM((assets, scenarios), BF16),
            pltpu.VMEM((assets, scenarios), BF16),
            pltpu.VMEM((scenarios, 2 * factors), BF16),
            pltpu.VMEM((DESKS, assets), BF16),
            pltpu.VMEM((assets, 128), F32),
            pltpu.VMEM((16, assets), BF16),
            pltpu.VMEM((n, 2, rows), F32),
            pltpu.VMEM((n, 2, rows), F32),
            pltpu.VMEM((n, 2, rows), F32),
            pltpu.VMEM((n, rows), F32),
            pltpu.VMEM((n, rows), F32),
            pltpu.VMEM((16, scenarios), BF16),
            pltpu.VMEM((n, 8, DESKS), F32),
            dma((2, last)),
            dma((2, last)),
            dma((2 * last + 1,)),
            dma((2 * last + 1,)),
            dma((n,)),
            dma((n,)),
            dma((n,)),
            dma((n,)),
            dma((n,)),
            dma((n,)),
            dma,
        ],
        compiler_params=pltpu.CompilerParams(
            collective_id=0, has_side_effects=True, vmem_limit_bytes=60 * 1024 * 1024
        ),
        name="tail_step",
    )(
        scen_draws,
        factor_mix,
        loadings,
        convexity.reshape(1, assets),
        holdings.reshape(1, assets),
        desk_map.reshape(1, assets),
        ranks.reshape(n, rows),
        desk_prices.reshape(1, DESKS),
    )
    return (allocation.reshape(DESKS), grad_load, grad_conv.reshape(assets))


def chip_distance(one, two):
    return sum(abs(a - b) for a, b in zip(one, two))


def ring_is_folded(mesh):
    try:
        places = [tuple(device.coords) for device in mesh.devices.reshape(-1, mesh.shape["asset"])[0]]
    except AttributeError:
        return False
    places = places[::2]
    chips = len(places)
    if chips % 2:
        return False
    costs = []
    for folded in (False, True):
        order = [places[chip_at(position, chips, folded)] for position in range(chips)]
        hops = [chip_distance(order[i], order[i + 1]) for i in range(chips - 1)]
        costs.append(sum(hops))
    return costs[1] < costs[0]


def solution(mesh):
    placed = (
        P(("groups", "asset"), None),
        P(),
        P(("groups", "asset"), None),
        P(("groups", "asset")),
        P(("groups", "asset")),
        P(("groups", "asset")),
        P("groups"),
        P("groups"),
    )
    return jax.shard_map(
        functools.partial(shards, ring_is_folded(mesh), mesh.shape["asset"]),
        mesh=mesh,
        in_specs=placed,
        out_specs=(P("groups"), P(("groups", "asset"), None), P(("groups", "asset"))),
        check_vma=False,
    )
```

```python
import functools
import math

import jax
import jax.numpy as jnp
from jax import lax
from jax.experimental import pallas as pl
from jax.experimental.pallas import tpu as pltpu
from jax.sharding import PartitionSpec as P

DESKS = 128
BAND = 32
CENTER = 166
PIECES = 4
MESH = pl.DeviceIdType.MESH
F32 = jnp.float32
BF16 = jnp.bfloat16
NT = (((1,), (1,)), ((), ()))


def dot(left, right):
    return jnp.dot(left, right, preferred_element_type=F32)


def dot_nt(left, right):
    return lax.dot_general(left, right, NT, preferred_element_type=F32)


def halves(value):
    high = value.astype(BF16).astype(F32)
    return high, value - high


def stack_rows(rows, count):
    width = rows[0].shape[1]
    if count > len(rows):
        rows = list(rows) + [jnp.zeros((count - len(rows), width), F32)]
    return jnp.concatenate(rows, axis=0)


def total(value):
    return jnp.sum(jnp.sum(value, axis=1, keepdims=True), axis=0, keepdims=True)


def position_of(chip, chips, folded):
    if not folded:
        return chip
    return chip // 2 + (chip % 2) * (chips - 1 - 2 * (chip // 2))


def chip_at(position, chips, folded):
    position = (position + chips) % chips
    if not folded:
        return position
    back = position // (chips // 2)
    return 2 * position + back * (2 * chips - 1 - 4 * position)


def kernel(
    n,
    folded,
    draws_ref,
    mix_hbm,
    load_hbm,
    conv_hbm,
    hold_hbm,
    desk_hbm,
    ranks_hbm,
    prices_hbm,
    final_ref,
    raw_hbm,
    raw_conv_hbm,
    mix_ref,
    load_ref,
    conv_ref,
    hold_ref,
    desk_ref,
    ranks_ref,
    prices_ref,
    grad_ref,
    gconv_ref,
    landed,
    shocks,
    tanhs,
    bends,
    scaled,
    table,
    columns,
    first_rows,
    part,
    gathered,
    sums,
    loss_all,
    valued_all,
    ranks_all,
    stat_rows,
    finals,
    ring_send,
    ring_recv,
    pair_send,
    pair_recv,
    part_send,
    part_recv,
    sums_send,
    sums_recv,
    fin_send,
    fin_recv,
    own_sem,
    in_sems,
    out_sems,
):
    me = lax.axis_index("asset")
    chips = n // 2
    core = me % 2
    chip = me // 2
    where = position_of(chip, chips, folded)
    partner = chip * 2 + (1 - core)
    right = chip_at(where + 1, chips, folded) * 2 + core
    left = chip_at(where - 1, chips, folded) * 2 + core
    rows, factors = draws_ref.shape
    block = 2 * rows
    scenarios = rows * n
    assets = load_ref.shape[0]
    tile = math.gcd(assets, 256)
    last = chips // 2
    part_rows = rows // PIECES

    barrier = pltpu.get_barrier_semaphore()
    for other in (right, left, partner):
        pl.semaphore_signal(barrier, inc=1, device_id={"asset": other}, device_id_type=MESH)
    own = pltpu.make_async_copy(draws_ref, landed.at[me], own_sem)
    own.start()
    inputs = [
        pltpu.make_async_copy(source, target, in_sems.at[index])
        for index, (source, target) in enumerate(
            [
                (conv_hbm, conv_ref),
                (hold_hbm, hold_ref),
                (desk_hbm, desk_ref),
                (prices_hbm, prices_ref),
                (load_hbm, load_ref),
                (mix_hbm, mix_ref),
                (ranks_hbm, ranks_ref),
            ]
        )
    ]
    for copy in inputs:
        copy.start()
    pl.semaphore_wait(barrier, 3)

    def shard_at(step):
        return chip_at(where + step, chips, folded) * 2 + core

    def ring_copy(direction, step, piece):
        shard = shard_at(-direction * (step - 1))
        lane = 0 if direction == 1 else 1
        span = pl.ds(piece * part_rows, part_rows)
        source = draws_ref.at[span] if step == 1 else landed.at[shard, span]
        return pltpu.make_async_remote_copy(
            src_ref=source,
            dst_ref=landed.at[shard, span],
            send_sem=ring_send.at[lane, step - 1, piece],
            recv_sem=ring_recv.at[lane, step - 1, piece],
            device_id={"asset": right if direction == 1 else left},
            device_id_type=MESH,
        )

    def pair_copy(step, piece):
        shard = shard_at(step)
        span = pl.ds(piece * part_rows, part_rows)
        source = draws_ref.at[span] if step == 0 else landed.at[shard, span]
        return pltpu.make_async_remote_copy(
            src_ref=source,
            dst_ref=landed.at[shard, span],
            send_sem=pair_send.at[step + last, piece],
            recv_sem=pair_recv.at[step + last, piece],
            device_id={"asset": partner},
            device_id_type=MESH,
        )

    started = []

    def start(copy):
        copy.start()
        started.append(copy)
        return copy

    def crossing(direction, step):
        if step < last:
            return range(PIECES)
        return range(PIECES // 2) if direction == 1 else range(PIECES // 2, PIECES)

    ring = {}
    pair = {}
    for piece in range(PIECES):
        for direction in (1, -1):
            if piece in crossing(direction, 1):
                ring[direction, 1, piece] = start(ring_copy(direction, 1, piece))
    for piece in range(PIECES):
        pair[0, piece] = start(pair_copy(0, piece))
    for copy in inputs:
        copy.wait()

    conv = conv_ref[...]
    hold = hold_ref[...]
    desk = desk_ref[...]
    same = lax.broadcasted_iota(jnp.int32, (DESKS, assets), 0) == desk
    table[...] = same.astype(F32).astype(BF16)
    price_high, price_rest = halves(prices_ref[...])
    price_mid, price_low = halves(price_rest)
    price_rows = stack_rows([price_high, price_mid, price_low], 16).astype(BF16)
    price = jnp.sum(dot(price_rows, table[...]), axis=0, keepdims=True)
    columns[...] = jnp.transpose(stack_rows([conv, hold, price], 128))
    linear = dot(
        stack_rows([*halves(hold), *halves(hold * price)], 16).astype(BF16), load_ref[...]
    )
    linear_loss = linear[0:1] + linear[1:2]
    linear_value = linear[2:3] + linear[3:4]
    linear_rows = stack_rows([*halves(linear_loss), *halves(linear_value)], 16).astype(BF16)
    bent = hold * conv
    first_rows[...] = stack_rows([*halves(bent), *halves(bent * price)], 16).astype(BF16)

    def forward(step):
        for piece in range(PIECES):
            pair[step, piece].wait_recv()
        place = chip_at(where + step, chips, folded)
        draws = landed[pl.ds(place * 2, 2)].reshape(block, factors)
        shock = dot(draws, mix_ref[...]).astype(BF16)
        at = pl.multiple_of(place * block, block)
        shocks[pl.ds(at, block), :] = shock
        result = dot_nt(linear_rows, shock)
        for first in range(0, assets, tile):
            exposure = dot_nt(load_ref[pl.ds(first, tile), :], shock)
            tanhs[pl.ds(first, tile), pl.ds(at, block)] = jnp.tanh(exposure).astype(BF16)
            size = jnp.abs(exposure)
            bend = (size + jnp.log(1.0 + jnp.exp(-2.0 * size)) - math.log(2.0)).astype(BF16)
            bends[pl.ds(first, tile), pl.ds(at, block)] = bend
            result = result + dot(first_rows[:, first : first + tile], bend)
            if first + tile < assets:
                yield
        loss = -(result[0:1] + result[1:2])
        value = result[2:3] + result[3:4]
        both = jnp.concatenate([loss, value], axis=0)
        part[place * 2] = both[:, 0:rows]
        part[place * 2 + 1] = both[:, rows:block]
        yield

    own.wait()
    parts = assets // tile
    pending = [0]
    for step in range(1, last + 1):
        work = [(running, index) for running in map(forward, pending) for index in range(parts)]
        slots = len(crossing(1, step))
        for slot in range(slots):
            for direction in (1, -1):
                piece = crossing(direction, step)[slot]
                ring[direction, step, piece].wait_recv()
                behind = -direction * step if step < last else last
                if step < last and piece in crossing(direction, step + 1):
                    ring[direction, step + 1, piece] = start(
                        ring_copy(direction, step + 1, piece)
                    )
                pair[behind, piece] = start(pair_copy(behind, piece))
            for running, index in work[: -(-len(work) // (slots - slot))]:
                next(running)
            work = work[-(-len(work) // (slots - slot)) :]
        pending = [-step, step] if step < last else [step]
    for running in map(forward, pending):
        for index in range(parts):
            next(running)
    for device in range(n):
        ranks_all[pl.ds(device, 1), :] = ranks_ref[:, device * rows : (device + 1) * rows]
    for copy in started:
        copy.wait_send()

    def to_all(source, target, send_sem, recv_sem):
        copies = []
        for offset in range(1, n):
            other = (me + offset) % n
            copies.append(
                pltpu.make_async_remote_copy(
                    src_ref=source(other),
                    dst_ref=target(offset),
                    send_sem=send_sem.at[offset],
                    recv_sem=recv_sem.at[offset],
                    device_id={"asset": other},
                    device_id_type=MESH,
                )
            )
        for copy in copies:
            copy.start()
        return copies

    copies = to_all(lambda other: part.at[other], lambda offset: gathered.at[offset], part_send, part_recv)
    mine = part[me]
    for copy in copies:
        copy.wait()
    for offset in range(1, n):
        mine = mine + gathered[offset]
    sums[me] = mine
    copies = to_all(lambda other: sums.at[me], lambda offset: sums.at[me], sums_send, sums_recv)
    for copy in copies:
        copy.wait()
    for device in range(n):
        entry = sums[device]
        loss_all[pl.ds(device, 1), :] = entry[0:1]
        valued_all[pl.ds(device, 1), :] = entry[1:2]

    losses = loss_all[...]
    valued = valued_all[...]
    offsets = (ranks_all[...].astype(F32) - CENTER) / BAND
    counter = (
        lax.broadcasted_iota(jnp.int32, (n, rows), 0) * rows
        + lax.broadcasted_iota(jnp.int32, (n, rows), 1)
    )
    every = (counter.astype(F32) - CENTER) / BAND
    bell = jnp.exp(-0.5 * offsets * offsets) / total(jnp.exp(-0.5 * every * every))
    quantile = total(bell * losses)
    centred = losses - total(losses) / scenarios
    smoothing = 0.3 * jnp.sqrt(total(centred * centred) / scenarios + 1e-06)
    scores = (losses - quantile) / smoothing
    weights = jax.nn.sigmoid(scores)
    weight_total = total(weights)
    objective = -total(weights * valued) / weight_total
    slopes = (-valued - objective) / weight_total * weights * (1.0 - weights)
    grad_quant = -total(slopes) / smoothing
    grad_band = -total(slopes * scores) / smoothing
    grad_loss = (
        slopes / smoothing
        + bell * grad_quant
        + grad_band * 0.09 * centred / (scenarios * smoothing)
    )
    share = weights * (scenarios / weight_total)
    grad_loss = scenarios * grad_loss

    wide = -(-rows // 128) * 128
    upright = stack_rows([share, grad_loss], -(-2 * n // 128) * 128)
    if wide > rows:
        upright = jnp.concatenate(
            [upright, jnp.zeros((upright.shape[0], wide - rows), F32)], axis=1
        )
    upright = jnp.transpose(upright)
    for device in range(n):
        piece = shocks[device * rows : (device + 1) * rows, :].astype(F32)
        for side in range(2):
            scale = upright[0:rows, side * n + device : side * n + device + 1]
            scaled[
                device * rows : (device + 1) * rows, side * factors : (side + 1) * factors
            ] = (piece * scale).astype(BF16)
    pieces = [*halves(share), *halves(grad_loss)]
    for place in range(chips):
        lines = [
            jnp.concatenate(
                [piece[2 * place : 2 * place + 1], piece[2 * place + 1 : 2 * place + 2]], axis=1
            )
            for piece in pieces
        ]
        stat_rows[:, place * block : (place + 1) * block] = stack_rows(lines, 16).astype(BF16)

    plain = dot(stat_rows[...], shocks[...])
    plain_share = plain[0:1] + plain[1:2]
    plain_loss = plain[2:3] + plain[3:4]
    plain_rows = stack_rows([*halves(plain_share)], 16).astype(BF16)

    results = []
    squares = jnp.zeros((1, 1), F32)
    allocation = jnp.zeros((1, DESKS), F32)
    for first in range(0, assets, tile):
        span = slice(first, first + tile)
        both = dot(tanhs[span, :], scaled[...])
        conv_column = columns[span, 0:1]
        hold_column = columns[span, 1:2]
        price_column = columns[span, 2:3]
        raw = -hold_column * (
            price_column * (plain_share + conv_column * both[:, 0:factors])
            + (plain_loss + conv_column * both[:, factors:])
        )
        grad_ref[span, :] = raw
        copy = pltpu.make_async_copy(
            grad_ref.at[pl.ds(first, tile)],
            raw_hbm.at[pl.ds(first, tile)],
            out_sems.at[first // tile],
        )
        copy.start()
        results.append(copy)
        squares = squares + total(raw * raw)
        sides = dot_nt(stat_rows[...], bends[span, :])
        side_share = sides[0:1] + sides[1:2]
        side_loss = sides[2:3] + sides[3:4]
        hold_row = hold_ref[:, span]
        raw_conv = -hold_row * (price[:, span] * side_share + side_loss)
        gconv_ref[:, span] = raw_conv
        squares = squares + total(raw_conv * raw_conv)
        linear_share = dot_nt(plain_rows, load_ref[span, :])
        using = hold_row * (
            linear_share[0:1] + linear_share[1:2] + conv_ref[:, span] * side_share
        )
        using_rows = stack_rows([*halves(using)], 16).astype(BF16)
        found = dot_nt(using_rows, table[:, span])
        allocation = allocation - (found[0:1] + found[1:2])
    finals[me] = stack_rows(
        [allocation * (1.0 / scenarios), jnp.broadcast_to(squares, (1, DESKS))], 8
    )
    copies = to_all(lambda other: finals.at[me], lambda offset: finals.at[me], fin_send, fin_recv)
    copy = pltpu.make_async_copy(gconv_ref, raw_conv_hbm, out_sems.at[assets // tile])
    copy.start()
    results.append(copy)
    for copy in copies + results:
        copy.wait()
    final = finals[0]
    for device in range(1, n):
        final = final + finals[device]
    final_ref[...] = final


def scale_kernel(entries, final_ref, raw_ref, raw_conv_ref, alloc_ref, grad_ref, gconv_ref):
    factor = lax.rsqrt(final_ref[1:2, 0:1] / entries + 1e-06)
    alloc_ref[...] = final_ref[0:1, :]
    gconv_ref[...] = raw_conv_ref[...] * factor
    grad_ref[...] = raw_ref[...] * factor


def shards(
    folded, n, scen_draws, factor_mix, loadings, convexity, holdings, desk_map, ranks, desk_prices
):
    rows, factors = scen_draws.shape
    assets = loadings.shape[0]
    scenarios = rows * n
    last = n // 4
    tiles = assets // math.gcd(assets, 256)
    dma = pltpu.SemaphoreType.DMA
    vmem = pl.BlockSpec(memory_space=pltpu.VMEM)
    anywhere = pl.BlockSpec(memory_space=pl.ANY)
    final, raw, raw_conv = pl.pallas_call(
        functools.partial(kernel, n, folded),
        out_shape=(
            jax.ShapeDtypeStruct((8, DESKS), F32),
            jax.ShapeDtypeStruct((assets, factors), F32),
            jax.ShapeDtypeStruct((1, assets), F32),
        ),
        in_specs=[anywhere] * 8,
        out_specs=(vmem, anywhere, anywhere),
        scratch_shapes=[
            pltpu.VMEM((factors, factors), BF16),
            pltpu.VMEM((assets, factors), BF16),
            pltpu.VMEM((1, assets), F32),
            pltpu.VMEM((1, assets), F32),
            pltpu.VMEM((1, assets), jnp.int32),
            pltpu.VMEM((1, scenarios), jnp.int32),
            pltpu.VMEM((1, DESKS), F32),
            pltpu.VMEM((assets, factors), F32),
            pltpu.VMEM((1, assets), F32),
            pltpu.VMEM((n, rows, factors), BF16),
            pltpu.VMEM((scenarios, factors), BF16),
            pltpu.VMEM((assets, scenarios), BF16),
            pltpu.VMEM((assets, scenarios), BF16),
            pltpu.VMEM((scenarios, 2 * factors), BF16),
            pltpu.VMEM((DESKS, assets), BF16),
            pltpu.VMEM((assets, 128), F32),
            pltpu.VMEM((16, assets), BF16),
            pltpu.VMEM((n, 2, rows), F32),
            pltpu.VMEM((n, 2, rows), F32),
            pltpu.VMEM((n, 2, rows), F32),
            pltpu.VMEM((n, rows), F32),
            pltpu.VMEM((n, rows), F32),
            pltpu.VMEM((n, rows), jnp.int32),
            pltpu.VMEM((16, scenarios), BF16),
            pltpu.VMEM((n, 8, DESKS), F32),
            dma((2, last, PIECES)),
            dma((2, last, PIECES)),
            dma((2 * last + 1, PIECES)),
            dma((2 * last + 1, PIECES)),
            dma((n,)),
            dma((n,)),
            dma((n,)),
            dma((n,)),
            dma((n,)),
            dma((n,)),
            dma,
            dma((7,)),
            dma((tiles + 1,)),
        ],
        compiler_params=pltpu.CompilerParams(
            collective_id=0, has_side_effects=True, vmem_limit_bytes=60 * 1024 * 1024
        ),
        name="tail_step",
    )(
        scen_draws,
        factor_mix,
        loadings,
        convexity.reshape(1, assets),
        holdings.reshape(1, assets),
        desk_map.reshape(1, assets),
        ranks.reshape(1, scenarios),
        desk_prices.reshape(1, DESKS),
    )
    entries = assets * n * (factors + 1)
    grid = 4
    small = pl.BlockSpec((1, assets), lambda i: (0, 0))
    wide = pl.BlockSpec((assets // grid, factors), lambda i: (i, 0))
    allocation, grad_load, grad_conv = pl.pallas_call(
        functools.partial(scale_kernel, entries),
        grid=(grid,),
        out_shape=(
            jax.ShapeDtypeStruct((1, DESKS), F32),
            jax.ShapeDtypeStruct((assets, factors), F32),
            jax.ShapeDtypeStruct((1, assets), F32),
        ),
        in_specs=[pl.BlockSpec((8, DESKS), lambda i: (0, 0)), wide, small],
        out_specs=(pl.BlockSpec((1, DESKS), lambda i: (0, 0)), wide, small),
        name="scale_step",
    )(final, raw, raw_conv)
    return (allocation.reshape(DESKS), grad_load, grad_conv.reshape(assets))


def chip_distance(one, two):
    return sum(abs(a - b) for a, b in zip(one, two))


def ring_is_folded(mesh):
    try:
        places = [tuple(device.coords) for device in mesh.devices.reshape(-1, mesh.shape["asset"])[0]]
    except AttributeError:
        return False
    places = places[::2]
    chips = len(places)
    if chips % 2:
        return False
    costs = []
    for folded in (False, True):
        order = [places[chip_at(position, chips, folded)] for position in range(chips)]
        hops = [chip_distance(order[i], order[i + 1]) for i in range(chips - 1)]
        costs.append(sum(hops))
    return costs[1] < costs[0]


def solution(mesh):
    placed = (
        P(("groups", "asset"), None),
        P(),
        P(("groups", "asset"), None),
        P(("groups", "asset")),
        P(("groups", "asset")),
        P(("groups", "asset")),
        P("groups"),
        P("groups"),
    )
    return jax.shard_map(
        functools.partial(shards, ring_is_folded(mesh), mesh.shape["asset"]),
        mesh=mesh,
        in_specs=placed,
        out_specs=(P("groups"), P(("groups", "asset"), None), P(("groups", "asset"))),
        check_vma=False,
    )
```

```python
import functools
import math

import jax
import jax.numpy as jnp
from jax import lax
from jax.experimental import pallas as pl
from jax.experimental.pallas import tpu as pltpu
from jax.sharding import PartitionSpec as P

DESKS = 128
BAND = 32
CENTER = 166
PIECES = 4
MESH = pl.DeviceIdType.MESH
F32 = jnp.float32
BF16 = jnp.bfloat16
NT = (((1,), (1,)), ((), ()))


def dot(left, right):
    return jnp.dot(left, right, preferred_element_type=F32)


def dot_nt(left, right):
    return lax.dot_general(left, right, NT, preferred_element_type=F32)


def halves(value):
    high = value.astype(BF16).astype(F32)
    return high, value - high


def stack_rows(rows, count):
    width = rows[0].shape[1]
    if count > len(rows):
        rows = list(rows) + [jnp.zeros((count - len(rows), width), F32)]
    return jnp.concatenate(rows, axis=0)


def total(value):
    return jnp.sum(jnp.sum(value, axis=1, keepdims=True), axis=0, keepdims=True)


def position_of(chip, chips, folded):
    if not folded:
        return chip
    return chip // 2 + (chip % 2) * (chips - 1 - 2 * (chip // 2))


def chip_at(position, chips, folded):
    position = (position + chips) % chips
    if not folded:
        return position
    back = position // (chips // 2)
    return 2 * position + back * (2 * chips - 1 - 4 * position)


def kernel(
    n,
    folded,
    draws_ref,
    mix_hbm,
    load_hbm,
    conv_hbm,
    hold_hbm,
    desk_hbm,
    ranks_hbm,
    prices_hbm,
    final_ref,
    raw_hbm,
    raw_conv_hbm,
    mix_ref,
    load_ref,
    conv_ref,
    hold_ref,
    desk_ref,
    ranks_ref,
    prices_ref,
    grad_ref,
    gconv_ref,
    landed,
    shocks,
    tanhs,
    bends,
    scaled,
    table,
    columns,
    first_rows,
    part,
    gathered,
    sums,
    loss_all,
    valued_all,
    ranks_all,
    stat_rows,
    finals,
    ring_send,
    ring_recv,
    pair_send,
    pair_recv,
    part_send,
    part_recv,
    sums_send,
    sums_recv,
    fin_send,
    fin_recv,
    own_sem,
    in_sems,
    out_sems,
):
    me = lax.axis_index("asset")
    chips = n // 2
    core = me % 2
    chip = me // 2
    where = position_of(chip, chips, folded)
    partner = chip * 2 + (1 - core)
    right = chip_at(where + 1, chips, folded) * 2 + core
    left = chip_at(where - 1, chips, folded) * 2 + core
    rows, factors = draws_ref.shape
    block = 2 * rows
    scenarios = rows * n
    assets = load_ref.shape[0]
    tile = math.gcd(assets, 256)
    last = chips // 2
    part_rows = rows // PIECES

    barrier = pltpu.get_barrier_semaphore()
    for other in (right, left, partner):
        pl.semaphore_signal(barrier, inc=1, device_id={"asset": other}, device_id_type=MESH)
    own = pltpu.make_async_copy(draws_ref, landed.at[me], own_sem)
    own.start()
    inputs = [
        pltpu.make_async_copy(source, target, in_sems.at[index])
        for index, (source, target) in enumerate(
            [
                (conv_hbm, conv_ref),
                (hold_hbm, hold_ref),
                (desk_hbm, desk_ref),
                (prices_hbm, prices_ref),
                (load_hbm, load_ref),
                (mix_hbm, mix_ref),
                (ranks_hbm, ranks_ref),
            ]
        )
    ]
    for copy in inputs:
        copy.start()
    pl.semaphore_wait(barrier, 3)

    def shard_at(step):
        return chip_at(where + step, chips, folded) * 2 + core

    def ring_copy(direction, step, piece):
        shard = shard_at(-direction * (step - 1))
        lane = 0 if direction == 1 else 1
        span = pl.ds(piece * part_rows, part_rows)
        source = draws_ref.at[span] if step == 1 else landed.at[shard, span]
        return pltpu.make_async_remote_copy(
            src_ref=source,
            dst_ref=landed.at[shard, span],
            send_sem=ring_send.at[lane, step - 1, piece],
            recv_sem=ring_recv.at[lane, step - 1, piece],
            device_id={"asset": right if direction == 1 else left},
            device_id_type=MESH,
        )

    def pair_copy(step, piece):
        shard = shard_at(step)
        span = pl.ds(piece * part_rows, part_rows)
        source = draws_ref.at[span] if step == 0 else landed.at[shard, span]
        return pltpu.make_async_remote_copy(
            src_ref=source,
            dst_ref=landed.at[shard, span],
            send_sem=pair_send.at[step + last, piece],
            recv_sem=pair_recv.at[step + last, piece],
            device_id={"asset": partner},
            device_id_type=MESH,
        )

    started = []

    def start(copy):
        copy.start()
        started.append(copy)
        return copy

    def crossing(direction, step):
        if step < last:
            return range(PIECES)
        return range(PIECES // 2) if direction == 1 else range(PIECES // 2, PIECES)

    ring = {}
    pair = {}
    for piece in range(PIECES):
        for direction in (1, -1):
            if piece in crossing(direction, 1):
                ring[direction, 1, piece] = start(ring_copy(direction, 1, piece))
    for piece in range(PIECES):
        pair[0, piece] = start(pair_copy(0, piece))
    for copy in inputs:
        copy.wait()

    conv = conv_ref[...]
    hold = hold_ref[...]
    desk = desk_ref[...]
    same = lax.broadcasted_iota(jnp.int32, (DESKS, assets), 0) == desk
    table[...] = same.astype(F32).astype(BF16)
    price_high, price_rest = halves(prices_ref[...])
    price_mid, price_low = halves(price_rest)
    price_rows = stack_rows([price_high, price_mid, price_low], 16).astype(BF16)
    price = jnp.sum(dot(price_rows, table[...]), axis=0, keepdims=True)
    columns[...] = jnp.transpose(stack_rows([conv, hold, price], 128))
    linear = dot(
        stack_rows([*halves(hold), *halves(hold * price)], 16).astype(BF16), load_ref[...]
    )
    linear_loss = linear[0:1] + linear[1:2]
    linear_value = linear[2:3] + linear[3:4]
    linear_rows = stack_rows([*halves(linear_loss), *halves(linear_value)], 16).astype(BF16)
    bent = hold * conv
    first_rows[...] = stack_rows([*halves(bent), *halves(bent * price)], 16).astype(BF16)

    def forward(step):
        for piece in range(PIECES):
            pair[step, piece].wait_recv()
        place = chip_at(where + step, chips, folded)
        draws = landed[pl.ds(place * 2, 2)].reshape(block, factors)
        shock = dot(draws, mix_ref[...]).astype(BF16)
        at = pl.multiple_of(place * block, block)
        shocks[pl.ds(at, block), :] = shock
        result = dot_nt(linear_rows, shock)
        for first in range(0, assets, tile):
            exposure = dot_nt(load_ref[pl.ds(first, tile), :], shock)
            tanhs[pl.ds(first, tile), pl.ds(at, block)] = jnp.tanh(exposure).astype(BF16)
            size = jnp.abs(exposure)
            bend = (size + jnp.log(1.0 + jnp.exp(-2.0 * size)) - math.log(2.0)).astype(BF16)
            bends[pl.ds(first, tile), pl.ds(at, block)] = bend
            result = result + dot(first_rows[:, first : first + tile], bend)
            if first + tile < assets:
                yield
        loss = -(result[0:1] + result[1:2])
        value = result[2:3] + result[3:4]
        both = jnp.concatenate([loss, value], axis=0)
        part[place * 2] = both[:, 0:rows]
        part[place * 2 + 1] = both[:, rows:block]
        yield

    own.wait()
    parts = assets // tile
    pending = [0]
    for step in range(1, last + 1):
        work = [(running, index) for running in map(forward, pending) for index in range(parts)]
        slots = len(crossing(1, step))
        for slot in range(slots):
            for direction in (1, -1):
                piece = crossing(direction, step)[slot]
                ring[direction, step, piece].wait_recv()
                behind = -direction * step if step < last else last
                if step < last and piece in crossing(direction, step + 1):
                    ring[direction, step + 1, piece] = start(
                        ring_copy(direction, step + 1, piece)
                    )
                pair[behind, piece] = start(pair_copy(behind, piece))
            for running, index in work[: -(-len(work) // (slots - slot))]:
                next(running)
            work = work[-(-len(work) // (slots - slot)) :]
        pending = [-step, step] if step < last else [step]
    for running in map(forward, pending):
        for index in range(parts):
            next(running)
    for device in range(n):
        ranks_all[pl.ds(device, 1), :] = ranks_ref[:, device * rows : (device + 1) * rows]
    for copy in started:
        copy.wait_send()

    def to_all(source, target, send_sem, recv_sem):
        copies = []
        for offset in range(1, n):
            other = (me + offset) % n
            copies.append(
                pltpu.make_async_remote_copy(
                    src_ref=source(other),
                    dst_ref=target(offset),
                    send_sem=send_sem.at[offset],
                    recv_sem=recv_sem.at[offset],
                    device_id={"asset": other},
                    device_id_type=MESH,
                )
            )
        for copy in copies:
            copy.start()
        return copies

    copies = to_all(lambda other: part.at[other], lambda offset: gathered.at[offset], part_send, part_recv)
    mine = part[me]
    for copy in copies:
        copy.wait()
    for offset in range(1, n):
        mine = mine + gathered[offset]
    sums[me] = mine
    copies = to_all(lambda other: sums.at[me], lambda offset: sums.at[me], sums_send, sums_recv)
    for copy in copies:
        copy.wait()
    for device in range(n):
        entry = sums[device]
        loss_all[pl.ds(device, 1), :] = entry[0:1]
        valued_all[pl.ds(device, 1), :] = entry[1:2]

    losses = loss_all[...]
    valued = valued_all[...]
    offsets = (ranks_all[...].astype(F32) - CENTER) / BAND
    counter = (
        lax.broadcasted_iota(jnp.int32, (n, rows), 0) * rows
        + lax.broadcasted_iota(jnp.int32, (n, rows), 1)
    )
    every = (counter.astype(F32) - CENTER) / BAND
    bell = jnp.exp(-0.5 * offsets * offsets) / total(jnp.exp(-0.5 * every * every))
    quantile = total(bell * losses)
    centred = losses - total(losses) / scenarios
    smoothing = 0.3 * jnp.sqrt(total(centred * centred) / scenarios + 1e-06)
    scores = (losses - quantile) / smoothing
    weights = jax.nn.sigmoid(scores)
    weight_total = total(weights)
    objective = -total(weights * valued) / weight_total
    slopes = (-valued - objective) / weight_total * weights * (1.0 - weights)
    grad_quant = -total(slopes) / smoothing
    grad_band = -total(slopes * scores) / smoothing
    grad_loss = (
        slopes / smoothing
        + bell * grad_quant
        + grad_band * 0.09 * centred / (scenarios * smoothing)
    )
    share = weights * (scenarios / weight_total)
    grad_loss = scenarios * grad_loss

    wide = -(-rows // 128) * 128
    upright = stack_rows([share, grad_loss], -(-2 * n // 128) * 128)
    if wide > rows:
        upright = jnp.concatenate(
            [upright, jnp.zeros((upright.shape[0], wide - rows), F32)], axis=1
        )
    upright = jnp.transpose(upright)
    for device in range(n):
        piece = shocks[device * rows : (device + 1) * rows, :].astype(F32)
        for side in range(2):
            scale = upright[0:rows, side * n + device : side * n + device + 1]
            scaled[
                device * rows : (device + 1) * rows, side * factors : (side + 1) * factors
            ] = (piece * scale).astype(BF16)
    pieces = [*halves(share), *halves(grad_loss)]
    for place in range(chips):
        lines = [
            jnp.concatenate(
                [piece[2 * place : 2 * place + 1], piece[2 * place + 1 : 2 * place + 2]], axis=1
            )
            for piece in pieces
        ]
        stat_rows[:, place * block : (place + 1) * block] = stack_rows(lines, 16).astype(BF16)

    plain = dot(stat_rows[...], shocks[...])
    plain_share = plain[0:1] + plain[1:2]
    plain_loss = plain[2:3] + plain[3:4]
    plain_rows = stack_rows([*halves(plain_share)], 16).astype(BF16)

    results = []
    squares = jnp.zeros((1, 1), F32)
    allocation = jnp.zeros((1, DESKS), F32)
    for first in range(0, assets, tile):
        span = slice(first, first + tile)
        both = dot(tanhs[span, :], scaled[...])
        conv_column = columns[span, 0:1]
        hold_column = columns[span, 1:2]
        price_column = columns[span, 2:3]
        raw = -hold_column * (
            price_column * (plain_share + conv_column * both[:, 0:factors])
            + (plain_loss + conv_column * both[:, factors:])
        )
        grad_ref[span, :] = raw
        copy = pltpu.make_async_copy(
            grad_ref.at[pl.ds(first, tile)],
            raw_hbm.at[pl.ds(first, tile)],
            out_sems.at[first // tile],
        )
        copy.start()
        results.append(copy)
        squares = squares + total(raw * raw)
        sides = dot_nt(stat_rows[...], bends[span, :])
        side_share = sides[0:1] + sides[1:2]
        side_loss = sides[2:3] + sides[3:4]
        hold_row = hold_ref[:, span]
        raw_conv = -hold_row * (price[:, span] * side_share + side_loss)
        gconv_ref[:, span] = raw_conv
        squares = squares + total(raw_conv * raw_conv)
        linear_share = dot_nt(plain_rows, load_ref[span, :])
        using = hold_row * (
            linear_share[0:1] + linear_share[1:2] + conv_ref[:, span] * side_share
        )
        using_rows = stack_rows([*halves(using)], 16).astype(BF16)
        found = dot_nt(using_rows, table[:, span])
        allocation = allocation - (found[0:1] + found[1:2])
    finals[me] = stack_rows(
        [allocation * (1.0 / scenarios), jnp.broadcast_to(squares, (1, DESKS))], 8
    )
    copies = to_all(lambda other: finals.at[me], lambda offset: finals.at[me], fin_send, fin_recv)
    copy = pltpu.make_async_copy(gconv_ref, raw_conv_hbm, out_sems.at[assets // tile])
    copy.start()
    results.append(copy)
    for copy in copies + results:
        copy.wait()
    final = finals[0]
    for device in range(1, n):
        final = final + finals[device]
    final_ref[...] = final


def scale_kernel(
    entries, final_ref, raw_conv_ref, raw_hbm, alloc_ref, gconv_ref, grad_hbm, held, in_sems, out_sems
):
    tile = held.shape[1]
    count = held.shape[0]
    reads = [
        pltpu.make_async_copy(raw_hbm.at[pl.ds(i * tile, tile)], held.at[i], in_sems.at[i])
        for i in range(count)
    ]
    for copy in reads:
        copy.start()
    factor = lax.rsqrt(final_ref[1:2, 0:1] / entries + 1e-06)
    alloc_ref[...] = final_ref[0:1, :]
    gconv_ref[...] = raw_conv_ref[...] * factor
    writes = []
    for i in range(count):
        reads[i].wait()
        held[i] = held[i] * factor
        copy = pltpu.make_async_copy(held.at[i], grad_hbm.at[pl.ds(i * tile, tile)], out_sems.at[i])
        copy.start()
        writes.append(copy)
    for copy in writes:
        copy.wait()


def shards(
    folded, n, scen_draws, factor_mix, loadings, convexity, holdings, desk_map, ranks, desk_prices
):
    rows, factors = scen_draws.shape
    assets = loadings.shape[0]
    scenarios = rows * n
    last = n // 4
    tiles = assets // math.gcd(assets, 256)
    dma = pltpu.SemaphoreType.DMA
    vmem = pl.BlockSpec(memory_space=pltpu.VMEM)
    anywhere = pl.BlockSpec(memory_space=pl.ANY)
    final, raw, raw_conv = pl.pallas_call(
        functools.partial(kernel, n, folded),
        out_shape=(
            jax.ShapeDtypeStruct((8, DESKS), F32),
            jax.ShapeDtypeStruct((assets, factors), F32),
            jax.ShapeDtypeStruct((1, assets), F32),
        ),
        in_specs=[anywhere] * 8,
        out_specs=(vmem, anywhere, anywhere),
        scratch_shapes=[
            pltpu.VMEM((factors, factors), BF16),
            pltpu.VMEM((assets, factors), BF16),
            pltpu.VMEM((1, assets), F32),
            pltpu.VMEM((1, assets), F32),
            pltpu.VMEM((1, assets), jnp.int32),
            pltpu.VMEM((1, scenarios), jnp.int32),
            pltpu.VMEM((1, DESKS), F32),
            pltpu.VMEM((assets, factors), F32),
            pltpu.VMEM((1, assets), F32),
            pltpu.VMEM((n, rows, factors), BF16),
            pltpu.VMEM((scenarios, factors), BF16),
            pltpu.VMEM((assets, scenarios), BF16),
            pltpu.VMEM((assets, scenarios), BF16),
            pltpu.VMEM((scenarios, 2 * factors), BF16),
            pltpu.VMEM((DESKS, assets), BF16),
            pltpu.VMEM((assets, 128), F32),
            pltpu.VMEM((16, assets), BF16),
            pltpu.VMEM((n, 2, rows), F32),
            pltpu.VMEM((n, 2, rows), F32),
            pltpu.VMEM((n, 2, rows), F32),
            pltpu.VMEM((n, rows), F32),
            pltpu.VMEM((n, rows), F32),
            pltpu.VMEM((n, rows), jnp.int32),
            pltpu.VMEM((16, scenarios), BF16),
            pltpu.VMEM((n, 8, DESKS), F32),
            dma((2, last, PIECES)),
            dma((2, last, PIECES)),
            dma((2 * last + 1, PIECES)),
            dma((2 * last + 1, PIECES)),
            dma((n,)),
            dma((n,)),
            dma((n,)),
            dma((n,)),
            dma((n,)),
            dma((n,)),
            dma,
            dma((7,)),
            dma((tiles + 1,)),
        ],
        compiler_params=pltpu.CompilerParams(
            collective_id=0, has_side_effects=True, vmem_limit_bytes=60 * 1024 * 1024
        ),
        name="tail_step",
    )(
        scen_draws,
        factor_mix,
        loadings,
        convexity.reshape(1, assets),
        holdings.reshape(1, assets),
        desk_map.reshape(1, assets),
        ranks.reshape(1, scenarios),
        desk_prices.reshape(1, DESKS),
    )
    entries = assets * n * (factors + 1)
    allocation, grad_conv, grad_load = pl.pallas_call(
        functools.partial(scale_kernel, entries),
        out_shape=(
            jax.ShapeDtypeStruct((1, DESKS), F32),
            jax.ShapeDtypeStruct((1, assets), F32),
            jax.ShapeDtypeStruct((assets, factors), F32),
        ),
        in_specs=[vmem, vmem, anywhere],
        out_specs=(vmem, vmem, anywhere),
        scratch_shapes=[
            pltpu.VMEM((tiles, assets // tiles, factors), F32),
            dma((tiles,)),
            dma((tiles,)),
        ],
        name="scale_step",
    )(final, raw_conv, raw)
    return (allocation.reshape(DESKS), grad_load, grad_conv.reshape(assets))


def chip_distance(one, two):
    return sum(abs(a - b) for a, b in zip(one, two))


def ring_is_folded(mesh):
    try:
        places = [tuple(device.coords) for device in mesh.devices.reshape(-1, mesh.shape["asset"])[0]]
    except AttributeError:
        return False
    places = places[::2]
    chips = len(places)
    if chips % 2:
        return False
    costs = []
    for folded in (False, True):
        order = [places[chip_at(position, chips, folded)] for position in range(chips)]
        hops = [chip_distance(order[i], order[i + 1]) for i in range(chips - 1)]
        costs.append(sum(hops))
    return costs[1] < costs[0]


def solution(mesh):
    placed = (
        P(("groups", "asset"), None),
        P(),
        P(("groups", "asset"), None),
        P(("groups", "asset")),
        P(("groups", "asset")),
        P(("groups", "asset")),
        P("groups"),
        P("groups"),
    )
    return jax.shard_map(
        functools.partial(shards, ring_is_folded(mesh), mesh.shape["asset"]),
        mesh=mesh,
        in_specs=placed,
        out_specs=(P("groups"), P(("groups", "asset"), None), P(("groups", "asset"))),
        check_vma=False,
    )
```

```python
import functools
import math

import jax
import jax.numpy as jnp
from jax import lax
from jax.experimental import pallas as pl
from jax.experimental.pallas import tpu as pltpu
from jax.sharding import PartitionSpec as P

DESKS = 128
BAND = 32
CENTER = 166
PIECES = 4
MESH = pl.DeviceIdType.MESH
F32 = jnp.float32
BF16 = jnp.bfloat16
NT = (((1,), (1,)), ((), ()))


def dot(left, right):
    return jnp.dot(left, right, preferred_element_type=F32)


def dot_nt(left, right):
    return lax.dot_general(left, right, NT, preferred_element_type=F32)


def halves(value):
    high = value.astype(BF16).astype(F32)
    return high, value - high


def stack_rows(rows, count):
    width = rows[0].shape[1]
    if count > len(rows):
        rows = list(rows) + [jnp.zeros((count - len(rows), width), F32)]
    return jnp.concatenate(rows, axis=0)


def total(value):
    return jnp.sum(jnp.sum(value, axis=1, keepdims=True), axis=0, keepdims=True)


def position_of(chip, chips, folded):
    if not folded:
        return chip
    return chip // 2 + (chip % 2) * (chips - 1 - 2 * (chip // 2))


def chip_at(position, chips, folded):
    position = (position + chips) % chips
    if not folded:
        return position
    back = position // (chips // 2)
    return 2 * position + back * (2 * chips - 1 - 4 * position)


def kernel(
    n,
    folded,
    draws_ref,
    mix_hbm,
    load_hbm,
    conv_hbm,
    hold_hbm,
    desk_hbm,
    ranks_hbm,
    prices_hbm,
    final_ref,
    raw_hbm,
    raw_conv_hbm,
    mix_ref,
    load_ref,
    conv_ref,
    hold_ref,
    desk_ref,
    ranks_ref,
    prices_ref,
    grad_ref,
    gconv_ref,
    landed,
    shocks,
    tanhs,
    bends,
    scaled,
    table,
    columns,
    first_rows,
    part,
    gathered,
    sums,
    loss_all,
    valued_all,
    ranks_all,
    stat_rows,
    finals,
    ring_send,
    ring_recv,
    pair_send,
    pair_recv,
    part_send,
    part_recv,
    sums_send,
    sums_recv,
    fin_send,
    fin_recv,
    own_sem,
    in_sems,
    out_sems,
):
    me = lax.axis_index("asset")
    chips = n // 2
    core = me % 2
    chip = me // 2
    where = position_of(chip, chips, folded)
    partner = chip * 2 + (1 - core)
    right = chip_at(where + 1, chips, folded) * 2 + core
    left = chip_at(where - 1, chips, folded) * 2 + core
    rows, factors = draws_ref.shape
    block = 2 * rows
    scenarios = rows * n
    assets = load_ref.shape[0]
    tile = math.gcd(assets, 256)
    last = chips // 2
    part_rows = rows // PIECES

    barrier = pltpu.get_barrier_semaphore()
    for other in (right, left, partner):
        pl.semaphore_signal(barrier, inc=1, device_id={"asset": other}, device_id_type=MESH)
    own = pltpu.make_async_copy(draws_ref, landed.at[me], own_sem)
    own.start()
    inputs = [
        pltpu.make_async_copy(source, target, in_sems.at[index])
        for index, (source, target) in enumerate(
            [
                (conv_hbm, conv_ref),
                (hold_hbm, hold_ref),
                (desk_hbm, desk_ref),
                (prices_hbm, prices_ref),
                (load_hbm, load_ref),
                (mix_hbm, mix_ref),
                (ranks_hbm, ranks_ref),
            ]
        )
    ]
    for copy in inputs:
        copy.start()
    pl.semaphore_wait(barrier, 3)

    def shard_at(step):
        return chip_at(where + step, chips, folded) * 2 + core

    def ring_copy(direction, step, piece):
        shard = shard_at(-direction * (step - 1))
        lane = 0 if direction == 1 else 1
        span = pl.ds(piece * part_rows, part_rows)
        source = draws_ref.at[span] if step == 1 else landed.at[shard, span]
        return pltpu.make_async_remote_copy(
            src_ref=source,
            dst_ref=landed.at[shard, span],
            send_sem=ring_send.at[lane, step - 1, piece],
            recv_sem=ring_recv.at[lane, step - 1, piece],
            device_id={"asset": right if direction == 1 else left},
            device_id_type=MESH,
        )

    def pair_copy(step, piece):
        shard = shard_at(step)
        span = pl.ds(piece * part_rows, part_rows)
        source = draws_ref.at[span] if step == 0 else landed.at[shard, span]
        return pltpu.make_async_remote_copy(
            src_ref=source,
            dst_ref=landed.at[shard, span],
            send_sem=pair_send.at[step + last, piece],
            recv_sem=pair_recv.at[step + last, piece],
            device_id={"asset": partner},
            device_id_type=MESH,
        )

    started = []

    def start(copy):
        copy.start()
        started.append(copy)
        return copy

    def crossing(direction, step):
        if step < last:
            return range(PIECES)
        return range(PIECES // 2) if direction == 1 else range(PIECES // 2, PIECES)

    ring = {}
    pair = {}
    for piece in range(PIECES):
        for direction in (1, -1):
            if piece in crossing(direction, 1):
                ring[direction, 1, piece] = start(ring_copy(direction, 1, piece))
    for piece in range(PIECES):
        pair[0, piece] = start(pair_copy(0, piece))
    for copy in inputs:
        copy.wait()

    conv = conv_ref[...]
    hold = hold_ref[...]
    desk = desk_ref[...]
    same = lax.broadcasted_iota(jnp.int32, (DESKS, assets), 0) == desk
    table[...] = same.astype(F32).astype(BF16)
    price_high, price_rest = halves(prices_ref[...])
    price_mid, price_low = halves(price_rest)
    price_rows = stack_rows([price_high, price_mid, price_low], 16).astype(BF16)
    price = jnp.sum(dot(price_rows, table[...]), axis=0, keepdims=True)
    columns[...] = jnp.transpose(stack_rows([conv, hold, price], 128))
    linear = dot(
        stack_rows([*halves(hold), *halves(hold * price)], 16).astype(BF16), load_ref[...]
    )
    linear_loss = linear[0:1] + linear[1:2]
    linear_value = linear[2:3] + linear[3:4]
    linear_rows = stack_rows([*halves(linear_loss), *halves(linear_value)], 16).astype(BF16)
    bent = hold * conv
    first_rows[...] = stack_rows([*halves(bent), *halves(bent * price)], 16).astype(BF16)

    parted = []

    def part_copy(other, offset):
        return pltpu.make_async_remote_copy(
            src_ref=part.at[other],
            dst_ref=gathered.at[offset],
            send_sem=part_send.at[offset],
            recv_sem=part_recv.at[offset],
            device_id={"asset": other},
            device_id_type=MESH,
        )

    def forward(step):
        for piece in range(PIECES):
            pair[step, piece].wait_recv()
        place = chip_at(where + step, chips, folded)
        draws = landed[pl.ds(place * 2, 2)].reshape(block, factors)
        shock = dot(draws, mix_ref[...]).astype(BF16)
        at = pl.multiple_of(place * block, block)
        shocks[pl.ds(at, block), :] = shock
        result = dot_nt(linear_rows, shock)
        for first in range(0, assets, tile):
            exposure = dot_nt(load_ref[pl.ds(first, tile), :], shock)
            tanhs[pl.ds(first, tile), pl.ds(at, block)] = jnp.tanh(exposure).astype(BF16)
            size = jnp.abs(exposure)
            bend = (size + jnp.log(1.0 + jnp.exp(-2.0 * size)) - math.log(2.0)).astype(BF16)
            bends[pl.ds(first, tile), pl.ds(at, block)] = bend
            result = result + dot(first_rows[:, first : first + tile], bend)
            if first + tile < assets:
                yield
        loss = -(result[0:1] + result[1:2])
        value = result[2:3] + result[3:4]
        both = jnp.concatenate([loss, value], axis=0)
        part[place * 2] = both[:, 0:rows]
        part[place * 2 + 1] = both[:, rows:block]
        for other in [partner] if step == 0 else [place * 2, place * 2 + 1]:
            copy = part_copy(other, (other - me + n) % n)
            copy.start()
            parted.append(copy)
        yield

    own.wait()
    parts = assets // tile
    pending = [0]
    for step in range(1, last + 1):
        work = [(running, index) for running in map(forward, pending) for index in range(parts)]
        slots = len(crossing(1, step))
        for slot in range(slots):
            for direction in (1, -1):
                piece = crossing(direction, step)[slot]
                ring[direction, step, piece].wait_recv()
                behind = -direction * step if step < last else last
                if step < last and piece in crossing(direction, step + 1):
                    ring[direction, step + 1, piece] = start(
                        ring_copy(direction, step + 1, piece)
                    )
                pair[behind, piece] = start(pair_copy(behind, piece))
            for running, index in work[: -(-len(work) // (slots - slot))]:
                next(running)
            work = work[-(-len(work) // (slots - slot)) :]
        pending = [-step, step] if step < last else [step]
    for running in map(forward, pending):
        for index in range(parts):
            next(running)
    for device in range(n):
        ranks_all[pl.ds(device, 1), :] = ranks_ref[:, device * rows : (device + 1) * rows]
    for copy in started:
        copy.wait_send()

    def to_all(source, target, send_sem, recv_sem):
        copies = []
        for offset in range(1, n):
            other = (me + offset) % n
            copies.append(
                pltpu.make_async_remote_copy(
                    src_ref=source(other),
                    dst_ref=target(offset),
                    send_sem=send_sem.at[offset],
                    recv_sem=recv_sem.at[offset],
                    device_id={"asset": other},
                    device_id_type=MESH,
                )
            )
        for copy in copies:
            copy.start()
        return copies

    mine = part[me]
    for offset in range(1, n):
        part_copy((me + offset) % n, offset).wait_recv()
    for copy in parted:
        copy.wait_send()
    for offset in range(1, n):
        mine = mine + gathered[offset]
    sums[me] = mine
    copies = to_all(lambda other: sums.at[me], lambda offset: sums.at[me], sums_send, sums_recv)
    for copy in copies:
        copy.wait()
    for device in range(n):
        entry = sums[device]
        loss_all[pl.ds(device, 1), :] = entry[0:1]
        valued_all[pl.ds(device, 1), :] = entry[1:2]

    losses = loss_all[...]
    valued = valued_all[...]
    offsets = (ranks_all[...].astype(F32) - CENTER) / BAND
    counter = (
        lax.broadcasted_iota(jnp.int32, (n, rows), 0) * rows
        + lax.broadcasted_iota(jnp.int32, (n, rows), 1)
    )
    every = (counter.astype(F32) - CENTER) / BAND
    bell = jnp.exp(-0.5 * offsets * offsets) / total(jnp.exp(-0.5 * every * every))
    quantile = total(bell * losses)
    centred = losses - total(losses) / scenarios
    smoothing = 0.3 * jnp.sqrt(total(centred * centred) / scenarios + 1e-06)
    scores = (losses - quantile) / smoothing
    weights = jax.nn.sigmoid(scores)
    weight_total = total(weights)
    objective = -total(weights * valued) / weight_total
    slopes = (-valued - objective) / weight_total * weights * (1.0 - weights)
    grad_quant = -total(slopes) / smoothing
    grad_band = -total(slopes * scores) / smoothing
    grad_loss = (
        slopes / smoothing
        + bell * grad_quant
        + grad_band * 0.09 * centred / (scenarios * smoothing)
    )
    share = weights * (scenarios / weight_total)
    grad_loss = scenarios * grad_loss

    wide = -(-rows // 128) * 128
    upright = stack_rows([share, grad_loss], -(-2 * n // 128) * 128)
    if wide > rows:
        upright = jnp.concatenate(
            [upright, jnp.zeros((upright.shape[0], wide - rows), F32)], axis=1
        )
    upright = jnp.transpose(upright)
    for device in range(n):
        piece = shocks[device * rows : (device + 1) * rows, :].astype(F32)
        for side in range(2):
            scale = upright[0:rows, side * n + device : side * n + device + 1]
            scaled[
                device * rows : (device + 1) * rows, side * factors : (side + 1) * factors
            ] = (piece * scale).astype(BF16)
    pieces = [*halves(share), *halves(grad_loss)]
    for place in range(chips):
        lines = [
            jnp.concatenate(
                [piece[2 * place : 2 * place + 1], piece[2 * place + 1 : 2 * place + 2]], axis=1
            )
            for piece in pieces
        ]
        stat_rows[:, place * block : (place + 1) * block] = stack_rows(lines, 16).astype(BF16)

    plain = dot(stat_rows[...], shocks[...])
    plain_share = plain[0:1] + plain[1:2]
    plain_loss = plain[2:3] + plain[3:4]
    plain_rows = stack_rows([*halves(plain_share)], 16).astype(BF16)

    results = []
    squares = jnp.zeros((1, 1), F32)
    allocation = jnp.zeros((1, DESKS), F32)
    for first in range(0, assets, tile):
        span = slice(first, first + tile)
        both = dot(tanhs[span, :], scaled[...])
        conv_column = columns[span, 0:1]
        hold_column = columns[span, 1:2]
        price_column = columns[span, 2:3]
        raw = -hold_column * (
            price_column * (plain_share + conv_column * both[:, 0:factors])
            + (plain_loss + conv_column * both[:, factors:])
        )
        grad_ref[span, :] = raw
        copy = pltpu.make_async_copy(
            grad_ref.at[pl.ds(first, tile)],
            raw_hbm.at[pl.ds(first, tile)],
            out_sems.at[first // tile],
        )
        copy.start()
        results.append(copy)
        squares = squares + total(raw * raw)
        sides = dot_nt(stat_rows[...], bends[span, :])
        side_share = sides[0:1] + sides[1:2]
        side_loss = sides[2:3] + sides[3:4]
        hold_row = hold_ref[:, span]
        raw_conv = -hold_row * (price[:, span] * side_share + side_loss)
        gconv_ref[:, span] = raw_conv
        squares = squares + total(raw_conv * raw_conv)
        linear_share = dot_nt(plain_rows, load_ref[span, :])
        using = hold_row * (
            linear_share[0:1] + linear_share[1:2] + conv_ref[:, span] * side_share
        )
        using_rows = stack_rows([*halves(using)], 16).astype(BF16)
        found = dot_nt(using_rows, table[:, span])
        allocation = allocation - (found[0:1] + found[1:2])
    finals[me] = stack_rows(
        [allocation * (1.0 / scenarios), jnp.broadcast_to(squares, (1, DESKS))], 8
    )
    copies = to_all(lambda other: finals.at[me], lambda offset: finals.at[me], fin_send, fin_recv)
    copy = pltpu.make_async_copy(gconv_ref, raw_conv_hbm, out_sems.at[assets // tile])
    copy.start()
    results.append(copy)
    for copy in copies + results:
        copy.wait()
    final = finals[0]
    for device in range(1, n):
        final = final + finals[device]
    final_ref[...] = final


def scale_kernel(entries, final_ref, raw_ref, raw_conv_ref, alloc_ref, grad_ref, gconv_ref):
    factor = lax.rsqrt(final_ref[1:2, 0:1] / entries + 1e-06)
    alloc_ref[...] = final_ref[0:1, :]
    gconv_ref[...] = raw_conv_ref[...] * factor
    grad_ref[...] = raw_ref[...] * factor


def shards(
    folded, n, scen_draws, factor_mix, loadings, convexity, holdings, desk_map, ranks, desk_prices
):
    rows, factors = scen_draws.shape
    assets = loadings.shape[0]
    scenarios = rows * n
    last = n // 4
    tiles = assets // math.gcd(assets, 256)
    dma = pltpu.SemaphoreType.DMA
    vmem = pl.BlockSpec(memory_space=pltpu.VMEM)
    anywhere = pl.BlockSpec(memory_space=pl.ANY)
    final, raw, raw_conv = pl.pallas_call(
        functools.partial(kernel, n, folded),
        out_shape=(
            jax.ShapeDtypeStruct((8, DESKS), F32),
            jax.ShapeDtypeStruct((assets, factors), F32),
            jax.ShapeDtypeStruct((1, assets), F32),
        ),
        in_specs=[anywhere] * 8,
        out_specs=(vmem, anywhere, anywhere),
        scratch_shapes=[
            pltpu.VMEM((factors, factors), BF16),
            pltpu.VMEM((assets, factors), BF16),
            pltpu.VMEM((1, assets), F32),
            pltpu.VMEM((1, assets), F32),
            pltpu.VMEM((1, assets), jnp.int32),
            pltpu.VMEM((1, scenarios), jnp.int32),
            pltpu.VMEM((1, DESKS), F32),
            pltpu.VMEM((assets, factors), F32),
            pltpu.VMEM((1, assets), F32),
            pltpu.VMEM((n, rows, factors), BF16),
            pltpu.VMEM((scenarios, factors), BF16),
            pltpu.VMEM((assets, scenarios), BF16),
            pltpu.VMEM((assets, scenarios), BF16),
            pltpu.VMEM((scenarios, 2 * factors), BF16),
            pltpu.VMEM((DESKS, assets), BF16),
            pltpu.VMEM((assets, 128), F32),
            pltpu.VMEM((16, assets), BF16),
            pltpu.VMEM((n, 2, rows), F32),
            pltpu.VMEM((n, 2, rows), F32),
            pltpu.VMEM((n, 2, rows), F32),
            pltpu.VMEM((n, rows), F32),
            pltpu.VMEM((n, rows), F32),
            pltpu.VMEM((n, rows), jnp.int32),
            pltpu.VMEM((16, scenarios), BF16),
            pltpu.VMEM((n, 8, DESKS), F32),
            dma((2, last, PIECES)),
            dma((2, last, PIECES)),
            dma((2 * last + 1, PIECES)),
            dma((2 * last + 1, PIECES)),
            dma((n,)),
            dma((n,)),
            dma((n,)),
            dma((n,)),
            dma((n,)),
            dma((n,)),
            dma,
            dma((7,)),
            dma((tiles + 1,)),
        ],
        compiler_params=pltpu.CompilerParams(
            collective_id=0, has_side_effects=True, vmem_limit_bytes=60 * 1024 * 1024
        ),
        name="tail_step",
    )(
        scen_draws,
        factor_mix,
        loadings,
        convexity.reshape(1, assets),
        holdings.reshape(1, assets),
        desk_map.reshape(1, assets),
        ranks.reshape(1, scenarios),
        desk_prices.reshape(1, DESKS),
    )
    entries = assets * n * (factors + 1)
    grid = 4
    small = pl.BlockSpec((1, assets), lambda i: (0, 0))
    wide = pl.BlockSpec((assets // grid, factors), lambda i: (i, 0))
    allocation, grad_load, grad_conv = pl.pallas_call(
        functools.partial(scale_kernel, entries),
        grid=(grid,),
        out_shape=(
            jax.ShapeDtypeStruct((1, DESKS), F32),
            jax.ShapeDtypeStruct((assets, factors), F32),
            jax.ShapeDtypeStruct((1, assets), F32),
        ),
        in_specs=[pl.BlockSpec((8, DESKS), lambda i: (0, 0)), wide, small],
        out_specs=(pl.BlockSpec((1, DESKS), lambda i: (0, 0)), wide, small),
        name="scale_step",
    )(final, raw, raw_conv)
    return (allocation.reshape(DESKS), grad_load, grad_conv.reshape(assets))


def chip_distance(one, two):
    return sum(abs(a - b) for a, b in zip(one, two))


def ring_is_folded(mesh):
    try:
        places = [tuple(device.coords) for device in mesh.devices.reshape(-1, mesh.shape["asset"])[0]]
    except AttributeError:
        return False
    places = places[::2]
    chips = len(places)
    if chips % 2:
        return False
    costs = []
    for folded in (False, True):
        order = [places[chip_at(position, chips, folded)] for position in range(chips)]
        hops = [chip_distance(order[i], order[i + 1]) for i in range(chips - 1)]
        costs.append(sum(hops))
    return costs[1] < costs[0]


def solution(mesh):
    placed = (
        P(("groups", "asset"), None),
        P(),
        P(("groups", "asset"), None),
        P(("groups", "asset")),
        P(("groups", "asset")),
        P(("groups", "asset")),
        P("groups"),
        P("groups"),
    )
    return jax.shard_map(
        functools.partial(shards, ring_is_folded(mesh), mesh.shape["asset"]),
        mesh=mesh,
        in_specs=placed,
        out_specs=(P("groups"), P(("groups", "asset"), None), P(("groups", "asset"))),
        check_vma=False,
    )
```
